32 devices in a mesh: gx: 4 (over z), gy: 8 (over y, x, core).
Axes of the slice: x: 2, y: 2, z: 4, core: 2. Of those that a mesh axis runs over, the one named last changes fastest.
Arguments:
- source: float32 [64, 256, 512], P('gx', 'gy')
- voxel_phase: int32 [64, 256, 512], P('gx', 'gy'), may hold values from 0 to 2
- lin_potential: float32 [64, 256, 512], P('gx', 'gy'), may hold values from -1 to 1
- link_voxel: int32 [4, 8, 2048], P('gx', 'gy'), may hold values from 0 to 262143
- link_count: int32 [4, 8, 8], P('gx', 'gy'), may hold values from 1 to 256, as said below
- link_target: int32 [4, 8, 2048], P('gx', 'gy'), may hold values from 0 to 511
Outputs:
- solution: float32 [64, 256, 512], P('gx', 'gy')
- particle_current: float32 [4, 8, 512], P('gx', 'gy')
The draws below stay inside these ranges and needn't reach their ends.
Inputs may be any that keep to these rules, and one draw needn't show every extreme that they name: `link_count`: every device has exactly 256 live links to at least one gy peer.
All inputs are finite; a program needn't handle non-finite values.
Results may differ from the reference program's by a relative error of at most 0.00012.
Values sent between devices are 32-bit elements; how exact they have to be, the bound alone decides.
A program may use at most 128 MiB of HBM per device.

```python
import jax
import jax.numpy as jnp

CX = 16
CY = 32
CZ = 512
ITERS = 12
CAP = 256
PART_DEV = 512
VOX = 262144
NX = 64
NY = 256
NZ = 512
N_GX = 4
N_GY = 8


def draw_source(key, part):
    first_key = jax.random.fold_in(key, 0)
    xcoord = jnp.arange(NX).astype(jnp.float32) / NX
    ycoord = jnp.arange(NY).astype(jnp.float32) / NY
    ramp = (1.0 + 2.0 * xcoord)[:, None, None] * (1.0 + ycoord)[None, :, None]
    rough = jax.random.normal(first_key, (NX, NY, NZ), jnp.float32)
    return ramp * rough


def draw_link_count(key, part):
    load_key, count_key, full_key = jax.random.split(key, 3)
    load = jax.random.randint(load_key, (N_GX, N_GY, 1), 2, 5)
    highest = CAP * load // 4
    counts = jax.random.randint(count_key, (N_GX, N_GY, N_GY), highest // 2, highest + 1)
    full_peer = jax.random.randint(full_key, (N_GX, N_GY, 1), 0, N_GY)
    peer_ids = jnp.arange(N_GY)[None, None, :]
    return jnp.where(peer_ids == full_peer, CAP, counts).astype(jnp.int32)


def touch_ends(values, key, low, top_value):
    spot = [jax.random.randint(jax.random.fold_in(key, axis), (), 0, length) for axis, length in enumerate(values.shape)]
    longest = values.shape.index(max(values.shape))
    next_to = spot[:longest] + [(spot[longest] + 1) % values.shape[longest]] + spot[longest + 1:]
    return values.at[tuple(spot)].set(low).at[tuple(next_to)].set(top_value)


def level_of(stream_key, dims, cuts, smallest, high):
    level, own = 1.0, jax.random.fold_in(stream_key, 6)
    for axis_at, blocks in cuts:
        steps = jnp.exp(jax.random.uniform(jax.random.fold_in(own, axis_at), (blocks,), jnp.float32, smallest / len(cuts), high / len(cuts)))
        level = level * jnp.repeat(steps, dims[axis_at] // blocks).reshape([-1 if axis == axis_at else 1 for axis in range(len(dims))])
    return level


def setup_inputs(seed: int = 0) -> dict:
    keys = jax.random.split(jax.random.key(seed), 7)
    source = draw_source(jax.random.fold_in(keys[6], 71), 0)
    voxel_phase = touch_ends(jax.random.randint(keys[1], (NX, NY, NZ), 0, 3), jax.random.fold_in(keys[1], 1), 0, 2).astype(jnp.int32)
    lin_potential = jnp.clip(jax.random.uniform(keys[2], (NX, NY, NZ), jnp.float32, -1.0, 1.0) * level_of(keys[2], (NX, NY, NZ), ((0, 4), (1, 8)), -0.4, 0.0), -1.0, 1.0)
    link_voxel = touch_ends(jax.random.randint(keys[3], (N_GX, N_GY, N_GY * CAP), 0, VOX), jax.random.fold_in(keys[3], 1), 0, VOX - 1).astype(jnp.int32)
    link_count = draw_link_count(jax.random.fold_in(keys[6], 71), 0)
    link_target = touch_ends(jax.random.randint(keys[5], (N_GX, N_GY, N_GY * CAP), 0, PART_DEV), jax.random.fold_in(keys[5], 1), 0, PART_DEV - 1).astype(jnp.int32)
    return dict(source=source, voxel_phase=voxel_phase, lin_potential=lin_potential, link_voxel=link_voxel, link_count=link_count, link_target=link_target)


def rate_of(voxel_phase):
    return jnp.where(voxel_phase == 1, 0.3, jnp.where(voxel_phase == 2, 0.08, 0.02)).astype(jnp.float32)


def butler(lin_potential):
    rising = jnp.exp(0.4 * lin_potential)
    falling = jnp.exp(-0.6 * lin_potential)
    return rising - falling, 0.4 * rising + 0.6 * falling


def operate_whole(values, diagonal):
    padded = jnp.pad(values, 1)
    beside = padded[2:, 1:-1, 1:-1] + padded[:-2, 1:-1, 1:-1]
    beside = beside + padded[1:-1, 2:, 1:-1] + padded[1:-1, :-2, 1:-1]
    beside = beside + padded[1:-1, 1:-1, 2:] + padded[1:-1, 1:-1, :-2]
    return diagonal * values - beside


def reference(source, voxel_phase, lin_potential, link_voxel, link_count, link_target):
    base, slope = butler(lin_potential)
    diagonal = 6.0 + rate_of(voxel_phase) * slope
    solution = jnp.zeros_like(source)
    residual = source
    precond = residual / diagonal
    direction = precond
    norm_now = jnp.sum(residual * precond)
    for iteration in range(ITERS):
        image = operate_whole(direction, diagonal)
        alpha = norm_now / jnp.sum(direction * image)
        solution = solution + alpha * direction
        residual = residual - alpha * image
        precond = residual / diagonal
        norm_next = jnp.sum(residual * precond)
        direction = precond + (norm_next / norm_now) * direction
        norm_now = norm_next
    current = base + slope * solution
    blocks = current.reshape(N_GX, CX, N_GY, CY, CZ).transpose(0, 2, 1, 3, 4).reshape(N_GX, N_GY, CX * CY * CZ)
    picked = jnp.take_along_axis(blocks, link_voxel.astype(jnp.int32), axis=2)
    slot_ids = jnp.arange(N_GY * CAP).astype(jnp.int32)
    peer_ids = slot_ids // CAP
    within = slot_ids % CAP
    live = within[None, None, :] < link_count[:, :, peer_ids]
    sent = jnp.where(live, 0.5 * picked, jnp.float32(0.0))
    received = sent.reshape(N_GX, N_GY, N_GY, CAP).transpose(0, 2, 1, 3).reshape(N_GX, N_GY, N_GY * CAP)

    def owner_sum(values, targets):
        return jax.ops.segment_sum(values, targets, num_segments=PART_DEV)

    particle_current = jax.vmap(jax.vmap(owner_sum))(received, link_target)
    return solution, particle_current
```

```python
import functools

import jax
import jax.numpy as jnp
import numpy as np
from jax import lax
from jax.experimental import pallas as pl
from jax.experimental.pallas import tpu as pltpu
from jax.sharding import PartitionSpec as P

ITERS = 12
HALF = ITERS // 2
PART_DEV = 512
ROWS = 16
RHS = 15
F32 = jnp.float32


def gram_maps():
    s = HALF

    def unit(size, at):
        out = np.zeros(size)
        out[at] = 1.0
        return out

    def own_moments(size, offset):
        moments = []
        for k in range(s):
            moments.append(2 * unit(size, offset + 2 * k + 1) - unit(size, offset + 1))
            moments.append(2 * unit(size, offset + 2 * k + 2) - unit(size, offset + 2))
        return moments

    def entry(m, j, k):
        a, b = j + k, abs(j - k)
        return 0.5 * (
            m[a] - 0.5 * (m[a + 1] + m[abs(a - 1)]) + m[b] - 0.5 * (m[b + 1] + m[abs(b - 1)])
        )

    n1 = 2 * s + 1
    first = np.zeros((n1, ROWS, 128))
    mu = own_moments(n1, 0)
    for j in range(s):
        first[:, j, RHS] = mu[j]
        for k in range(s):
            first[:, j, k] = entry(mu, j, k)
    n2 = 4 * s + 1
    size = n2 + n1
    om = own_moments(size, 0)
    mu = own_moments(size, n2)
    nu = [unit(size, n1 + m) for m in range(s)]
    nu.append(unit(size, n1 + s))
    for j in range(1, s):
        nu.append(2 * unit(size, n1 + s + j) - nu[s - j])
    second = np.zeros((size, ROWS, 128))
    for j in range(s):
        second[:, j, RHS] = nu[j]
        second[:, s + j, RHS] = om[j]
        for k in range(s):
            second[:, j, k] = entry(mu, j, k)
            second[:, s + j, s + k] = entry(om, j, k)
            second[:, j, s + k] = entry(nu, j, k)
            second[:, s + j, k] = entry(nu, j, k)
    return first.astype(np.float32), second.astype(np.float32)


def solve(matrix, count):
    rows = lax.broadcasted_iota(jnp.int32, matrix.shape, 0)
    lanes = lax.broadcasted_iota(jnp.int32, matrix.shape, 1)
    for j in range(count):
        inverse = 1.0 / matrix[j : j + 1, j : j + 1]
        factor = jnp.where(rows == j, 0.0, matrix[:, j : j + 1] * inverse)
        matrix = matrix - factor * matrix[j : j + 1, :]
    pivots = jnp.sum(jnp.where(rows == lanes, matrix, 0.0), axis=1, keepdims=True)
    answer = matrix[:, RHS : RHS + 1] / pivots
    return [jnp.broadcast_to(answer[j : j + 1, :], (8, 128)) for j in range(count)]


def kernel(
    sizes, source, phase, potential, first_map, second_map, out,
    vecs, diag, inv, xhalo, yhalo, ybuf, dots, mine, parts,
    hsend, hrecv, rsend, rrecv,
):
    n_gx, n_gy = sizes
    total = n_gx * n_gy
    cx, cy, cz = source.shape
    s = HALF
    gx, gy = lax.axis_index("gx"), lax.axis_index("gy")
    me = gx * n_gy + gy
    mesh_id = pl.DeviceIdType.MESH

    barrier = pltpu.get_barrier_semaphore()

    @pl.loop(1, total)
    def _(step):
        t = lax.rem(me + step, total)
        pl.semaphore_signal(
            barrier, inc=1, device_id=(t // n_gy, lax.rem(t, n_gy)), device_id_type=mesh_id
        )

    zero_plane = jnp.zeros((cy, cz), F32)
    dots[...] = jnp.zeros(dots.shape, F32)

    @pl.when(gy == 0)
    def _():
        yhalo[:, 0] = jnp.zeros((yhalo.shape[0],) + yhalo.shape[2:], F32)

    @pl.when(gy == n_gy - 1)
    def _():
        yhalo[:, 1] = jnp.zeros((yhalo.shape[0],) + yhalo.shape[2:], F32)

    @pl.loop(0, cx)
    def _(x):
        rising = jnp.exp(0.4 * potential[x])
        falling = jnp.exp(-0.6 * potential[x])
        label = phase[x]
        rate = jnp.where(label == 1, 0.3, jnp.where(label == 2, 0.08, 0.02)).astype(F32)
        d = 6.0 + rate * (0.4 * rising + 0.6 * falling)
        i = 1.0 / d
        diag[x] = d
        inv[x] = i
        v = source[x] * i
        vecs[0, x] = zero_plane
        vecs[s + 2, x] = zero_plane
        vecs[1, x] = v
        ybuf[1, 0, pl.ds(x, 1), :] = v[0:1, :]
        ybuf[1, 1, pl.ds(x, 1), :] = v[cy - 1 : cy, :]

    pl.semaphore_wait(barrier, total - 1)

    def copies(at):
        def make(src, dst, way, target):
            return pltpu.make_async_remote_copy(
                src_ref=src, dst_ref=dst, send_sem=hsend.at[at, way],
                recv_sem=hrecv.at[at, way], device_id=target, device_id_type=mesh_id,
            )

        up = make(vecs.at[at, cx - 1], xhalo.at[at, 0], 0, (jnp.minimum(gx + 1, n_gx - 1), gy))
        down = make(vecs.at[at, 0], xhalo.at[at, 1], 1, (jnp.maximum(gx - 1, 0), gy))
        right = make(ybuf.at[at, 1], yhalo.at[at, 0], 2, (gx, jnp.minimum(gy + 1, n_gy - 1)))
        left = make(ybuf.at[at, 0], yhalo.at[at, 1], 3, (gx, jnp.maximum(gy - 1, 0)))
        return up, down, right, left

    has_up, has_down = gx < n_gx - 1, gx > 0
    has_right, has_left = gy < n_gy - 1, gy > 0
    sends = (has_up, has_down, has_right, has_left)
    takes = (has_down, has_up, has_left, has_right)

    zlane = lax.broadcasted_iota(jnp.int32, (cy, cz), 1)
    ysub = lax.broadcasted_iota(jnp.int32, (cy, cz), 0)

    def folded(product):
        return jnp.sum(product.reshape(cy // 8, 8, cz), axis=0)

    def chain_step(base, k, second):
        now = base + 1 + k
        scale = jnp.where(k == 0, 1.0, 2.0).astype(F32)
        moves = copies(now)
        for move, there in zip(moves, sends):
            pl.when(there)(move.start)

        def plane(x, carry, low, high):
            c = vecs[now, x]
            before = vecs[now - 1, x]
            n = jnp.where(zlane == 0, 0.0, pltpu.roll(c, 1, 1))
            n = n + jnp.where(zlane == cz - 1, 0.0, pltpu.roll(c, cz - 1, 1))
            n = n + jnp.where(ysub == 0, 0.0, pltpu.roll(c, 1, 0))
            n = n + jnp.where(ysub == cy - 1, 0.0, pltpu.roll(c, cy - 1, 0))
            if low:
                n = n + vecs[now, x - 1]
            if high:
                n = n + vecs[now, x + 1]
            vecs[now + 1, x] = (scale * inv[x]) * n - before
            weighted = diag[x] * c
            found = [weighted * c, weighted * before]
            if second:
                found.append(weighted * vecs[s + 1, x])
                found.append(diag[x] * vecs[s + 3, x] * vecs[1 + k, x])
            return tuple(a + folded(b) for a, b in zip(carry, found))

        carry = tuple(jnp.zeros((8, cz), F32) for _ in range(4 if second else 2))
        carry = plane(0, carry, False, True)
        carry = lax.fori_loop(1, cx - 1, lambda x, a: plane(x, a, True, True), carry)
        carry = plane(cx - 1, carry, True, False)
        dots[2 * k + 1] = carry[0]
        dots[2 * k] = carry[1]
        if second:
            dots[3 * s + 1 + k] = carry[2]
            dots[2 * s + 1 + k] = carry[3]

        for way in (2, 3):
            pl.when(takes[way])(moves[way].wait_recv)

        @pl.when(takes[0])
        def _():
            moves[0].wait_recv()
            vecs[now + 1, 0] = vecs[now + 1, 0] + (scale * inv[0]) * xhalo[now, 0]

        @pl.when(takes[1])
        def _():
            moves[1].wait_recv()
            vecs[now + 1, cx - 1] = (
                vecs[now + 1, cx - 1] + (scale * inv[cx - 1]) * xhalo[now, 1]
            )

        for x in range(cx):
            for side, y in ((0, 0), (1, cy - 1)):
                row = vecs[now + 1, x, y : y + 1, :] + (
                    scale * inv[x, y : y + 1, :]
                ) * yhalo[now, side, x : x + 1, :]
                vecs[now + 1, x, y : y + 1, :] = row
                ybuf[now + 1, side, x : x + 1, :] = row
        for move, there in zip(moves, sends):
            pl.when(there)(move.wait_send)

    def run_chain(base, second):
        @pl.loop(0, s)
        def _(k):
            chain_step(base, k, second)

        def last(x, a):
            return a + folded(diag[x] * vecs[base + s, x] * vecs[base + s + 1, x])

        dots[2 * s] = lax.fori_loop(0, cx, last, jnp.zeros((8, cz), F32))

    def reduced(which):
        part = jnp.sum(dots[...], axis=1)
        part = sum(part[:, 128 * z : 128 * (z + 1)] for z in range(cz // 128))
        part = jnp.sum(part, axis=1, keepdims=True)
        rows = lax.broadcasted_iota(jnp.int32, (dots.shape[0], 128), 0)
        lanes = lax.broadcasted_iota(jnp.int32, (dots.shape[0], 128), 1)
        row = jnp.sum(jnp.where(rows == lanes, part, 0.0), axis=0, keepdims=True)
        mine[which] = row
        parts[which, me] = row

        def move(owner, target):
            return pltpu.make_async_remote_copy(
                src_ref=mine.at[which], dst_ref=parts.at[which, owner],
                send_sem=rsend.at[which, target], recv_sem=rrecv.at[which, owner],
                device_id=(target // n_gy, lax.rem(target, n_gy)), device_id_type=mesh_id,
            )

        @pl.loop(1, total)
        def _(step):
            move(me, lax.rem(me + step, total)).start()

        @pl.loop(1, total)
        def _(step):
            other = lax.rem(me + step, total)
            move(other, other).wait_recv()

        @pl.loop(1, total)
        def _(step):
            move(me, lax.rem(me + step, total)).wait_send()

        return jnp.sum(parts[which], axis=0)

    def assembled(table, values):
        return sum(
            table[m] * jnp.broadcast_to(values[m][0][:, values[m][1] : values[m][1] + 1], (ROWS, 128))
            for m in range(table.shape[0])
        )

    def combine(coefficients, slots, store):
        @pl.loop(0, cx)
        def _(x):
            for y in range(0, cy, 8):
                for z in range(0, cz, 128):
                    pieces = [
                        w * vecs[slot, x, y : y + 8, z : z + 128]
                        for w, slot in zip(coefficients, slots)
                    ]
                    while len(pieces) > 1:
                        pieces = [sum(pieces[i : i + 2]) for i in range(0, len(pieces), 2)]
                    store(x, y, z, pieces[0])

    run_chain(0, False)
    sums = reduced(0)
    n1, n2 = 2 * s + 1, 4 * s + 1
    first = solve(assembled(first_map, [(sums, m) for m in range(n1)]), s)
    tail = [jnp.ones((8, 128), F32)] + [jnp.zeros((8, 128), F32) for _ in range(s)]
    for k in range(s):
        tail[k] = tail[k] - first[k]
        tail[k + 1] = tail[k + 1] + 0.5 * first[k]
        tail[abs(k - 1)] = tail[abs(k - 1)] + 0.5 * first[k]
    base = s + 2

    def keep(x, y, z, value):
        vecs[base + 1, x, y : y + 8, z : z + 128] = value

    combine(tail, range(1, s + 2), keep)
    for x in range(cx):
        ybuf[base + 1, 0, x : x + 1, :] = vecs[base + 1, x, 0:1, :]
        ybuf[base + 1, 1, x : x + 1, :] = vecs[base + 1, x, cy - 1 : cy, :]
    run_chain(base, True)
    again = reduced(1)
    values = [(again, m) for m in range(n2)] + [(sums, m) for m in range(n1)]
    second = solve(assembled(second_map, values), 2 * s)
    weights = [first[k] + second[k] for k in range(s)] + second[s:]

    def emit(x, y, z, value):
        out[x, y : y + 8, z : z + 128] = value

    combine(weights, list(range(1, s + 1)) + list(range(base + 1, base + s + 1)), emit)


def solved(sizes, source, voxel_phase, lin_potential):
    cx, cy, cz = source.shape
    total = sizes[0] * sizes[1]
    slots = 2 * HALF + 4
    first_map, second_map = gram_maps()
    lanes = 4 * HALF + 8
    whole = pl.BlockSpec(memory_space=pltpu.VMEM)
    return pl.pallas_call(
        functools.partial(kernel, sizes),
        out_shape=jax.ShapeDtypeStruct(source.shape, F32),
        in_specs=[whole] * 5,
        out_specs=whole,
        scratch_shapes=[
            pltpu.VMEM((slots, cx, cy, cz), F32),
            pltpu.VMEM((cx, cy, cz), F32),
            pltpu.VMEM((cx, cy, cz), F32),
            pltpu.VMEM((slots, 2, cy, cz), F32),
            pltpu.VMEM((slots, 2, cx, cz), F32),
            pltpu.VMEM((slots, 2, cx, cz), F32),
            pltpu.VMEM((lanes, 8, cz), F32),
            pltpu.VMEM((2, 1, 128), F32),
            pltpu.VMEM((2, total, 1, 128), F32),
            pltpu.SemaphoreType.DMA((slots, 4)),
            pltpu.SemaphoreType.DMA((slots, 4)),
            pltpu.SemaphoreType.DMA((2, total)),
            pltpu.SemaphoreType.DMA((2, total)),
        ],
        compiler_params=pltpu.CompilerParams(collective_id=0, has_side_effects=True),
    )(source, voxel_phase, lin_potential, jnp.asarray(first_map), jnp.asarray(second_map))


def butler(lin_potential):
    rising = jnp.exp(0.4 * lin_potential)
    falling = jnp.exp(-0.6 * lin_potential)
    return (rising - falling, 0.4 * rising + 0.6 * falling)


def shards(sizes, source, voxel_phase, lin_potential, link_voxel, link_count, link_target):
    solution = solved(sizes, source, voxel_phase, lin_potential)
    at = link_voxel[0, 0]
    base, slope = butler(lin_potential.reshape(-1)[at])
    current = base + slope * solution.reshape(-1)[at]
    peers = link_count.shape[2]
    capacity = link_voxel.shape[2] // peers
    picked = current.reshape(peers, capacity)
    within = jnp.arange(capacity)
    live = within[None, :] < link_count[0, 0][:, None]
    outgoing = jnp.where(live, 0.5 * picked, jnp.float32(0.0))
    incoming = lax.all_to_all(outgoing, "gy", split_axis=0, concat_axis=0, tiled=True)
    totals = jax.ops.segment_sum(incoming.reshape(-1), link_target[0, 0], num_segments=PART_DEV)
    return (solution, totals.reshape(1, 1, PART_DEV))


def solution(mesh):
    spec = P("gx", "gy", None)
    return jax.shard_map(
        functools.partial(shards, (mesh.shape["gx"], mesh.shape["gy"])),
        mesh=mesh,
        in_specs=(spec,) * 6,
        out_specs=(spec, spec),
        check_vma=False,
    )
```

```python
import functools

import jax
import jax.numpy as jnp
import numpy as np
from jax import lax
from jax.experimental import pallas as pl
from jax.experimental.pallas import tpu as pltpu
from jax.sharding import PartitionSpec as P

ITERS = 12
HALF = ITERS // 2
PART_DEV = 512
ROWS = 16
RHS = 15
F32 = jnp.float32


def gram_maps():
    s = HALF

    def unit(size, at):
        out = np.zeros(size)
        out[at] = 1.0
        return out

    def own_moments(size, offset):
        moments = []
        for k in range(s):
            moments.append(2 * unit(size, offset + 2 * k + 1) - unit(size, offset + 1))
            moments.append(2 * unit(size, offset + 2 * k + 2) - unit(size, offset + 2))
        return moments

    def entry(m, j, k):
        a, b = j + k, abs(j - k)
        return 0.5 * (
            m[a] - 0.5 * (m[a + 1] + m[abs(a - 1)]) + m[b] - 0.5 * (m[b + 1] + m[abs(b - 1)])
        )

    n1 = 2 * s + 1
    first = np.zeros((n1, ROWS, 128))
    mu = own_moments(n1, 0)
    for j in range(s):
        first[:, j, RHS] = mu[j]
        for k in range(s):
            first[:, j, k] = entry(mu, j, k)
    n2 = 4 * s + 1
    size = n2 + n1
    om = own_moments(size, 0)
    mu = own_moments(size, n2)
    nu = [unit(size, n1 + m) for m in range(s)]
    nu.append(unit(size, n1 + s))
    for j in range(1, s):
        nu.append(2 * unit(size, n1 + s + j) - nu[s - j])
    second = np.zeros((size, ROWS, 128))
    for j in range(s):
        second[:, j, RHS] = nu[j]
        second[:, s + j, RHS] = om[j]
        for k in range(s):
            second[:, j, k] = entry(mu, j, k)
            second[:, s + j, s + k] = entry(om, j, k)
            second[:, j, s + k] = entry(nu, j, k)
            second[:, s + j, k] = entry(nu, j, k)
    return first.astype(np.float32), second.astype(np.float32)


def solve(matrix, count):
    rows = lax.broadcasted_iota(jnp.int32, matrix.shape, 0)
    lanes = lax.broadcasted_iota(jnp.int32, matrix.shape, 1)
    for j in range(count):
        inverse = 1.0 / matrix[j : j + 1, j : j + 1]
        factor = jnp.where(rows == j, 0.0, matrix[:, j : j + 1] * inverse)
        matrix = matrix - factor * matrix[j : j + 1, :]
    pivots = jnp.sum(jnp.where(rows == lanes, matrix, 0.0), axis=1, keepdims=True)
    answer = matrix[:, RHS : RHS + 1] / pivots
    return [jnp.broadcast_to(answer[j : j + 1, :], (8, 128)) for j in range(count)]


def kernel(
    sizes, source, phase, potential, first_map, second_map, voxel, count, target, out, particle,
    vecs, diag, inv, xhalo, yhalo, ybuf, dots, mine, parts, pick, level, sent, got,
    hsend, hrecv, rsend, rrecv, lsend, lrecv,
):
    n_gx, n_gy = sizes
    total = n_gx * n_gy
    cx, cy, cz = source.shape
    s = HALF
    gx, gy = lax.axis_index("gx"), lax.axis_index("gy")
    me = gx * n_gy + gy
    mesh_id = pl.DeviceIdType.MESH

    barrier = pltpu.get_barrier_semaphore()

    @pl.loop(1, total)
    def _(step):
        t = lax.rem(me + step, total)
        pl.semaphore_signal(
            barrier, inc=1, device_id=(t // n_gy, lax.rem(t, n_gy)), device_id_type=mesh_id
        )

    zero_plane = jnp.zeros((cy, cz), F32)
    dots[...] = jnp.zeros(dots.shape, F32)

    @pl.when(gy == 0)
    def _():
        yhalo[:, 0] = jnp.zeros((yhalo.shape[0],) + yhalo.shape[2:], F32)

    @pl.when(gy == n_gy - 1)
    def _():
        yhalo[:, 1] = jnp.zeros((yhalo.shape[0],) + yhalo.shape[2:], F32)

    @pl.loop(0, cx)
    def _(x):
        rising = jnp.exp(0.4 * potential[x])
        falling = jnp.exp(-0.6 * potential[x])
        label = phase[x]
        rate = jnp.where(label == 1, 0.3, jnp.where(label == 2, 0.08, 0.02)).astype(F32)
        d = 6.0 + rate * (0.4 * rising + 0.6 * falling)
        i = 1.0 / d
        diag[x] = d
        inv[x] = i
        v = source[x] * i
        vecs[0, x] = zero_plane
        vecs[s + 2, x] = zero_plane
        vecs[1, x] = v
        ybuf[1, 0, pl.ds(x, 1), :] = v[0:1, :]
        ybuf[1, 1, pl.ds(x, 1), :] = v[cy - 1 : cy, :]

    pl.semaphore_wait(barrier, total - 1)

    def copies(at):
        def make(src, dst, way, target):
            return pltpu.make_async_remote_copy(
                src_ref=src, dst_ref=dst, send_sem=hsend.at[at, way],
                recv_sem=hrecv.at[at, way], device_id=target, device_id_type=mesh_id,
            )

        up = make(vecs.at[at, cx - 1], xhalo.at[at, 0], 0, (jnp.minimum(gx + 1, n_gx - 1), gy))
        down = make(vecs.at[at, 0], xhalo.at[at, 1], 1, (jnp.maximum(gx - 1, 0), gy))
        right = make(ybuf.at[at, 1], yhalo.at[at, 0], 2, (gx, jnp.minimum(gy + 1, n_gy - 1)))
        left = make(ybuf.at[at, 0], yhalo.at[at, 1], 3, (gx, jnp.maximum(gy - 1, 0)))
        return up, down, right, left

    has_up, has_down = gx < n_gx - 1, gx > 0
    has_right, has_left = gy < n_gy - 1, gy > 0
    sends = (has_up, has_down, has_right, has_left)
    takes = (has_down, has_up, has_left, has_right)

    zlane = lax.broadcasted_iota(jnp.int32, (cy, cz), 1)
    ysub = lax.broadcasted_iota(jnp.int32, (cy, cz), 0)

    def folded(product):
        return jnp.sum(product.reshape(cy // 8, 8, cz), axis=0)

    def chain_step(base, k, second):
        now = base + 1 + k
        scale = jnp.where(k == 0, 1.0, 2.0).astype(F32)
        moves = copies(now)
        for move, there in zip(moves, sends):
            pl.when(there)(move.start)

        def plane(x, carry, low, high):
            c = vecs[now, x]
            before = vecs[now - 1, x]
            n = jnp.where(zlane == 0, 0.0, pltpu.roll(c, 1, 1))
            n = n + jnp.where(zlane == cz - 1, 0.0, pltpu.roll(c, cz - 1, 1))
            n = n + jnp.where(ysub == 0, 0.0, pltpu.roll(c, 1, 0))
            n = n + jnp.where(ysub == cy - 1, 0.0, pltpu.roll(c, cy - 1, 0))
            if low:
                n = n + vecs[now, x - 1]
            if high:
                n = n + vecs[now, x + 1]
            vecs[now + 1, x] = (scale * inv[x]) * n - before
            weighted = diag[x] * c
            found = [weighted * c, weighted * before]
            if second:
                found.append(weighted * vecs[s + 1, x])
                found.append(diag[x] * vecs[s + 3, x] * vecs[1 + k, x])
            return tuple(a + folded(b) for a, b in zip(carry, found))

        carry = tuple(jnp.zeros((8, cz), F32) for _ in range(4 if second else 2))
        carry = plane(0, carry, False, True)
        carry = lax.fori_loop(1, cx - 1, lambda x, a: plane(x, a, True, True), carry)
        carry = plane(cx - 1, carry, True, False)
        dots[2 * k + 1] = carry[0]
        dots[2 * k] = carry[1]
        if second:
            dots[3 * s + 1 + k] = carry[2]
            dots[2 * s + 1 + k] = carry[3]

        for way in (2, 3):
            pl.when(takes[way])(moves[way].wait_recv)

        @pl.when(takes[0])
        def _():
            moves[0].wait_recv()
            vecs[now + 1, 0] = vecs[now + 1, 0] + (scale * inv[0]) * xhalo[now, 0]

        @pl.when(takes[1])
        def _():
            moves[1].wait_recv()
            vecs[now + 1, cx - 1] = (
                vecs[now + 1, cx - 1] + (scale * inv[cx - 1]) * xhalo[now, 1]
            )

        for x in range(cx):
            for side, y in ((0, 0), (1, cy - 1)):
                row = vecs[now + 1, x, y : y + 1, :] + (
                    scale * inv[x, y : y + 1, :]
                ) * yhalo[now, side, x : x + 1, :]
                vecs[now + 1, x, y : y + 1, :] = row
                ybuf[now + 1, side, x : x + 1, :] = row
        for move, there in zip(moves, sends):
            pl.when(there)(move.wait_send)

    def run_chain(base, second):
        @pl.loop(0, s)
        def _(k):
            chain_step(base, k, second)

        def last(x, a):
            return a + folded(diag[x] * vecs[base + s, x] * vecs[base + s + 1, x])

        dots[2 * s] = lax.fori_loop(0, cx, last, jnp.zeros((8, cz), F32))

    groups = target.shape[0]
    wide = groups // n_gy
    lane = lax.broadcasted_iota(jnp.int32, (1, 128), 1)
    zbits, ybits = cz.bit_length() - 1, cy.bit_length() - 1

    def gathered(ref, group):
        @pl.loop(0, 128, step=16)
        def _(start):
            for i in range(16):
                v = voxel[group * 128 + start + i]
                row = ref[v >> (zbits + ybits), pl.ds((v >> zbits) & (cy - 1), 1), :]
                spot = v & (cz - 1)
                kept = jnp.zeros((1, 128), F32)
                for z in range(0, cz, 128):
                    kept = jnp.where(lane == spot - z, row[:, z : z + 128], kept)
                pick[pl.ds(start + i, 1), :] = kept

        return jnp.sum(pick[...].T, axis=0, keepdims=True)

    def levels(start, stop):
        @pl.loop(start, stop)
        def _(group):
            level[pl.ds(group, 1), :] = gathered(potential, group)

    def reduced(which, meanwhile):
        part = jnp.sum(dots[...], axis=1)
        part = sum(part[:, 128 * z : 128 * (z + 1)] for z in range(cz // 128))
        part = jnp.sum(part, axis=1, keepdims=True)
        rows = lax.broadcasted_iota(jnp.int32, (dots.shape[0], 128), 0)
        lanes = lax.broadcasted_iota(jnp.int32, (dots.shape[0], 128), 1)
        row = jnp.sum(jnp.where(rows == lanes, part, 0.0), axis=0, keepdims=True)
        mine[which] = row
        parts[which, me] = row

        def move(owner, target):
            return pltpu.make_async_remote_copy(
                src_ref=mine.at[which], dst_ref=parts.at[which, owner],
                send_sem=rsend.at[which, target], recv_sem=rrecv.at[which, owner],
                device_id=(target // n_gy, lax.rem(target, n_gy)), device_id_type=mesh_id,
            )

        @pl.loop(1, total)
        def _(step):
            move(me, lax.rem(me + step, total)).start()

        meanwhile()

        @pl.loop(1, total)
        def _(step):
            other = lax.rem(me + step, total)
            move(other, other).wait_recv()

        @pl.loop(1, total)
        def _(step):
            move(me, lax.rem(me + step, total)).wait_send()

        return jnp.sum(parts[which], axis=0)

    def assembled(table, values):
        return sum(
            table[m] * jnp.broadcast_to(values[m][0][:, values[m][1] : values[m][1] + 1], (ROWS, 128))
            for m in range(table.shape[0])
        )

    def combine(coefficients, slots, store):
        @pl.loop(0, cx)
        def _(x):
            for y in range(0, cy, 8):
                for z in range(0, cz, 128):
                    pieces = [
                        w * vecs[slot, x, y : y + 8, z : z + 128]
                        for w, slot in zip(coefficients, slots)
                    ]
                    while len(pieces) > 1:
                        pieces = [sum(pieces[i : i + 2]) for i in range(0, len(pieces), 2)]
                    store(x, y, z, pieces[0])

    run_chain(0, False)
    sums = reduced(0, lambda: levels(0, groups // 2))
    n1, n2 = 2 * s + 1, 4 * s + 1
    first = solve(assembled(first_map, [(sums, m) for m in range(n1)]), s)
    tail = [jnp.ones((8, 128), F32)] + [jnp.zeros((8, 128), F32) for _ in range(s)]
    for k in range(s):
        tail[k] = tail[k] - first[k]
        tail[k + 1] = tail[k + 1] + 0.5 * first[k]
        tail[abs(k - 1)] = tail[abs(k - 1)] + 0.5 * first[k]
    base = s + 2

    def keep(x, y, z, value):
        vecs[base + 1, x, y : y + 8, z : z + 128] = value

    combine(tail, range(1, s + 2), keep)
    for x in range(cx):
        ybuf[base + 1, 0, x : x + 1, :] = vecs[base + 1, x, 0:1, :]
        ybuf[base + 1, 1, x : x + 1, :] = vecs[base + 1, x, cy - 1 : cy, :]
    run_chain(base, True)
    again = reduced(1, lambda: levels(groups // 2, groups))
    values = [(again, m) for m in range(n2)] + [(sums, m) for m in range(n1)]
    second = solve(assembled(second_map, values), 2 * s)
    weights = [first[k] + second[k] for k in range(s)] + second[s:]

    def emit(x, y, z, value):
        out[x, y : y + 8, z : z + 128] = value

    combine(weights, list(range(1, s + 1)) + list(range(base + 1, base + s + 1)), emit)

    @pl.loop(0, n_gy)
    def _(peer):
        live = count[peer]
        for part in range(wide):
            group = peer * wide + part
            at = level[pl.ds(group, 1), :]
            rising = jnp.exp(0.4 * at)
            falling = jnp.exp(-0.6 * at)
            slope = 0.4 * rising + 0.6 * falling
            current = (rising - falling) + slope * gathered(out, group)
            sent[peer, part : part + 1, :] = jnp.where(
                lane + 128 * part < live, 0.5 * current, 0.0
            )

    def link(owner, peer):
        return pltpu.make_async_remote_copy(
            src_ref=sent.at[peer], dst_ref=got.at[owner], send_sem=lsend.at[peer],
            recv_sem=lrecv.at[owner], device_id=(gx, peer), device_id_type=mesh_id,
        )

    @pl.loop(1, n_gy)
    def _(step):
        link(gy, lax.rem(gy + step, n_gy)).start()

    got[gy] = sent[gy]

    @pl.loop(1, n_gy)
    def _(step):
        other = lax.rem(gy + step, n_gy)
        link(other, other).wait_recv()

    own = particle.shape[1]
    sub = lax.broadcasted_iota(jnp.int32, (128, 128), 0)
    for start in range(0, own, 128):
        def add(peer, acc):
            for part in range(wide):
                spot = target[pl.ds(peer * wide + part, 1), :]
                acc = acc + jnp.where(spot - start == sub, got[peer, part : part + 1, :], 0.0)
            return acc

        acc = lax.fori_loop(0, n_gy, add, jnp.zeros((128, 128), F32))
        particle[:, start : start + 128] = jnp.sum(acc.T, axis=0, keepdims=True)

    @pl.loop(1, n_gy)
    def _(step):
        link(gy, lax.rem(gy + step, n_gy)).wait_send()


def shards(sizes, source, voxel_phase, lin_potential, link_voxel, link_count, link_target):
    cx, cy, cz = source.shape
    total = sizes[0] * sizes[1]
    slots = 2 * HALF + 4
    first_map, second_map = gram_maps()
    lanes = 4 * HALF + 8
    whole = pl.BlockSpec(memory_space=pltpu.VMEM)
    peers = link_count.shape[2]
    groups = link_voxel.shape[2] // 128
    scalars = pl.BlockSpec(memory_space=pltpu.SMEM)
    values, totals = pl.pallas_call(
        functools.partial(kernel, sizes),
        out_shape=(
            jax.ShapeDtypeStruct(source.shape, F32),
            jax.ShapeDtypeStruct((1, PART_DEV), F32),
        ),
        in_specs=[whole] * 5 + [scalars, scalars, whole],
        out_specs=(whole, whole),
        scratch_shapes=[
            pltpu.VMEM((slots, cx, cy, cz), F32),
            pltpu.VMEM((cx, cy, cz), F32),
            pltpu.VMEM((cx, cy, cz), F32),
            pltpu.VMEM((slots, 2, cy, cz), F32),
            pltpu.VMEM((slots, 2, cx, cz), F32),
            pltpu.VMEM((slots, 2, cx, cz), F32),
            pltpu.VMEM((lanes, 8, cz), F32),
            pltpu.VMEM((2, 1, 128), F32),
            pltpu.VMEM((2, total, 1, 128), F32),
            pltpu.VMEM((128, 128), F32),
            pltpu.VMEM((groups, 128), F32),
            pltpu.VMEM((peers, groups // peers, 128), F32),
            pltpu.VMEM((peers, groups // peers, 128), F32),
            pltpu.SemaphoreType.DMA((slots, 4)),
            pltpu.SemaphoreType.DMA((slots, 4)),
            pltpu.SemaphoreType.DMA((2, total)),
            pltpu.SemaphoreType.DMA((2, total)),
            pltpu.SemaphoreType.DMA((peers,)),
            pltpu.SemaphoreType.DMA((peers,)),
        ],
        compiler_params=pltpu.CompilerParams(collective_id=0, has_side_effects=True),
    )(
        source, voxel_phase, lin_potential, jnp.asarray(first_map), jnp.asarray(second_map),
        link_voxel[0, 0], link_count[0, 0], link_target[0, 0].reshape(groups, 128),
    )
    return values, totals.reshape(1, 1, PART_DEV)


def solution(mesh):
    spec = P("gx", "gy", None)
    return jax.shard_map(
        functools.partial(shards, (mesh.shape["gx"], mesh.shape["gy"])),
        mesh=mesh,
        in_specs=(spec,) * 6,
        out_specs=(spec, spec),
        check_vma=False,
    )
```

```python
import functools

import jax
import jax.numpy as jnp
import numpy as np
from jax import lax
from jax.experimental import pallas as pl
from jax.experimental.pallas import tpu as pltpu
from jax.sharding import PartitionSpec as P

ITERS = 12
HALF = ITERS // 2
PART_DEV = 512
ROWS = 16
RHS = 15
F32 = jnp.float32


def gram_maps():
    s = HALF

    def unit(size, at):
        out = np.zeros(size)
        out[at] = 1.0
        return out

    def own_moments(size, offset):
        moments = []
        for k in range(s):
            moments.append(2 * unit(size, offset + 2 * k + 1) - unit(size, offset + 1))
            moments.append(2 * unit(size, offset + 2 * k + 2) - unit(size, offset + 2))
        return moments

    def entry(m, j, k):
        a, b = j + k, abs(j - k)
        return 0.5 * (
            m[a] - 0.5 * (m[a + 1] + m[abs(a - 1)]) + m[b] - 0.5 * (m[b + 1] + m[abs(b - 1)])
        )

    n1 = 2 * s + 1
    first = np.zeros((n1, ROWS, 128))
    mu = own_moments(n1, 0)
    for j in range(s):
        first[:, j, RHS] = mu[j]
        for k in range(s):
            first[:, j, k] = entry(mu, j, k)
    n2 = 4 * s + 1
    size = n2 + n1
    om = own_moments(size, 0)
    mu = own_moments(size, n2)
    nu = [unit(size, n1 + m) for m in range(s)]
    nu.append(unit(size, n1 + s))
    for j in range(1, s):
        nu.append(2 * unit(size, n1 + s + j) - nu[s - j])
    second = np.zeros((size, ROWS, 128))
    for j in range(s):
        second[:, j, RHS] = nu[j]
        second[:, s + j, RHS] = om[j]
        for k in range(s):
            second[:, j, k] = entry(mu, j, k)
            second[:, s + j, s + k] = entry(om, j, k)
            second[:, j, s + k] = entry(nu, j, k)
            second[:, s + j, k] = entry(nu, j, k)
    return first.astype(np.float32), second.astype(np.float32)


def solve(matrix, count):
    rows = lax.broadcasted_iota(jnp.int32, matrix.shape, 0)
    lanes = lax.broadcasted_iota(jnp.int32, matrix.shape, 1)
    for j in range(count):
        inverse = 1.0 / matrix[j : j + 1, j : j + 1]
        factor = jnp.where(rows == j, 0.0, matrix[:, j : j + 1] * inverse)
        matrix = matrix - factor * matrix[j : j + 1, :]
    pivots = jnp.sum(jnp.where(rows == lanes, matrix, 0.0), axis=1, keepdims=True)
    answer = matrix[:, RHS : RHS + 1] / pivots
    return [jnp.broadcast_to(answer[j : j + 1, :], (8, 128)) for j in range(count)]


def kernel(
    sizes, source, phase, potential, first_map, second_map, voxel, count, target, out, particle,
    vecs, diag, inv, xhalo, yhalo, ybuf, dots, mine, parts, pick, flat, level, sent, got,
    hsend, hrecv, rsend, rrecv, lsend, lrecv,
):
    n_gx, n_gy = sizes
    total = n_gx * n_gy
    cx, cy, cz = source.shape
    s = HALF
    gx, gy = lax.axis_index("gx"), lax.axis_index("gy")
    me = gx * n_gy + gy
    mesh_id = pl.DeviceIdType.MESH

    barrier = pltpu.get_barrier_semaphore()

    @pl.loop(1, total)
    def _(step):
        t = lax.rem(me + step, total)
        pl.semaphore_signal(
            barrier, inc=1, device_id=(t // n_gy, lax.rem(t, n_gy)), device_id_type=mesh_id
        )

    zero_plane = jnp.zeros((cy, cz), F32)
    dots[...] = jnp.zeros(dots.shape, F32)

    @pl.when(gy == 0)
    def _():
        yhalo[:, 0] = jnp.zeros((yhalo.shape[0],) + yhalo.shape[2:], F32)

    @pl.when(gy == n_gy - 1)
    def _():
        yhalo[:, 1] = jnp.zeros((yhalo.shape[0],) + yhalo.shape[2:], F32)

    @pl.loop(0, cx)
    def _(x):
        rising = jnp.exp(0.4 * potential[x])
        falling = jnp.exp(-0.6 * potential[x])
        label = phase[x]
        rate = jnp.where(label == 1, 0.3, jnp.where(label == 2, 0.08, 0.02)).astype(F32)
        d = 6.0 + rate * (0.4 * rising + 0.6 * falling)
        i = 1.0 / d
        diag[x] = d
        inv[x] = i
        v = source[x] * i
        vecs[0, x] = zero_plane
        vecs[s + 2, x] = zero_plane
        vecs[1, x] = v
        ybuf[1, 0, pl.ds(x, 1), :] = v[0:1, :]
        ybuf[1, 1, pl.ds(x, 1), :] = v[cy - 1 : cy, :]

    def copies(at):
        def make(src, dst, way, target):
            return pltpu.make_async_remote_copy(
                src_ref=src, dst_ref=dst, send_sem=hsend.at[at, way],
                recv_sem=hrecv.at[at, way], device_id=target, device_id_type=mesh_id,
            )

        up = make(vecs.at[at, cx - 1], xhalo.at[at, 0], 0, (jnp.minimum(gx + 1, n_gx - 1), gy))
        down = make(vecs.at[at, 0], xhalo.at[at, 1], 1, (jnp.maximum(gx - 1, 0), gy))
        right = make(ybuf.at[at, 1], yhalo.at[at, 0], 2, (gx, jnp.minimum(gy + 1, n_gy - 1)))
        left = make(ybuf.at[at, 0], yhalo.at[at, 1], 3, (gx, jnp.maximum(gy - 1, 0)))
        return up, down, right, left

    has_up, has_down = gx < n_gx - 1, gx > 0
    has_right, has_left = gy < n_gy - 1, gy > 0
    sends = (has_up, has_down, has_right, has_left)
    takes = (has_down, has_up, has_left, has_right)

    zlane = lax.broadcasted_iota(jnp.int32, (cy, cz), 1)
    ysub = lax.broadcasted_iota(jnp.int32, (cy, cz), 0)

    def folded(product):
        return jnp.sum(product.reshape(cy // 8, 8, cz), axis=0)

    def chain_step(base, k, second):
        now = base + 1 + k
        scale = jnp.where(k == 0, 1.0, 2.0).astype(F32)
        moves = copies(now)
        for move, there in zip(moves, sends):
            pl.when(there)(move.start)

        def plane(x, carry, low, high):
            c = vecs[now, x]
            before = vecs[now - 1, x]
            n = jnp.where(zlane == 0, 0.0, pltpu.roll(c, 1, 1))
            n = n + jnp.where(zlane == cz - 1, 0.0, pltpu.roll(c, cz - 1, 1))
            n = n + jnp.where(ysub == 0, 0.0, pltpu.roll(c, 1, 0))
            n = n + jnp.where(ysub == cy - 1, 0.0, pltpu.roll(c, cy - 1, 0))
            if low:
                n = n + vecs[now, x - 1]
            if high:
                n = n + vecs[now, x + 1]
            vecs[now + 1, x] = (scale * inv[x]) * n - before
            weighted = diag[x] * c
            found = [weighted * c, weighted * before]
            if second:
                found.append(weighted * vecs[s + 1, x])
                found.append(diag[x] * vecs[s + 3, x] * vecs[1 + k, x])
            return tuple(a + folded(b) for a, b in zip(carry, found))

        carry = tuple(jnp.zeros((8, cz), F32) for _ in range(4 if second else 2))
        carry = plane(0, carry, False, True)
        carry = lax.fori_loop(1, cx - 1, lambda x, a: plane(x, a, True, True), carry)
        carry = plane(cx - 1, carry, True, False)
        dots[2 * k + 1] = carry[0]
        dots[2 * k] = carry[1]
        if second:
            dots[3 * s + 1 + k] = carry[2]
            dots[2 * s + 1 + k] = carry[3]

        for way in (2, 3):
            pl.when(takes[way])(moves[way].wait_recv)

        @pl.when(takes[0])
        def _():
            moves[0].wait_recv()
            vecs[now + 1, 0] = vecs[now + 1, 0] + (scale * inv[0]) * xhalo[now, 0]

        @pl.when(takes[1])
        def _():
            moves[1].wait_recv()
            vecs[now + 1, cx - 1] = (
                vecs[now + 1, cx - 1] + (scale * inv[cx - 1]) * xhalo[now, 1]
            )

        for x in range(cx):
            for side, y in ((0, 0), (1, cy - 1)):
                row = vecs[now + 1, x, y : y + 1, :] + (
                    scale * inv[x, y : y + 1, :]
                ) * yhalo[now, side, x : x + 1, :]
                vecs[now + 1, x, y : y + 1, :] = row
                ybuf[now + 1, side, x : x + 1, :] = row
        for move, there in zip(moves, sends):
            pl.when(there)(move.wait_send)

    def run_chain(base, second):
        @pl.loop(0, s)
        def _(k):
            chain_step(base, k, second)

        def last(x, a):
            return a + folded(diag[x] * vecs[base + s, x] * vecs[base + s + 1, x])

        dots[2 * s] = lax.fori_loop(0, cx, last, jnp.zeros((8, cz), F32))

    groups = target.shape[0]
    wide = groups // n_gy
    tiles = cz // 128
    lane = lax.broadcasted_iota(jnp.int32, (1, 128), 1)

    def gathered(ref, group):
        @pl.loop(0, 128, step=32)
        def _(start):
            for i in range(32):
                v = voxel[group * 128 + start + i]
                row = ref[pl.ds(v >> 7, 1), :]
                pick[pl.ds(start + i, 1), :] = jnp.where(lane == (v & 127), row, 0.0)

        return jnp.sum(pick[...].T, axis=0, keepdims=True)

    def flatten(x, y, z, value):
        start = (x * cy + y) * tiles + z // 128
        flat[pl.ds(start, 8, stride=tiles), :] = value

    def levels(start, stop):
        @pl.loop(start, stop)
        def _(group):
            level[pl.ds(group, 1), :] = gathered(flat, group)

    def reduced(which, meanwhile):
        part = jnp.sum(dots[...], axis=1)
        part = sum(part[:, 128 * z : 128 * (z + 1)] for z in range(cz // 128))
        part = jnp.sum(part, axis=1, keepdims=True)
        rows = lax.broadcasted_iota(jnp.int32, (dots.shape[0], 128), 0)
        lanes = lax.broadcasted_iota(jnp.int32, (dots.shape[0], 128), 1)
        row = jnp.sum(jnp.where(rows == lanes, part, 0.0), axis=0, keepdims=True)
        mine[which] = row
        parts[which, me] = row

        def move(owner, target):
            return pltpu.make_async_remote_copy(
                src_ref=mine.at[which], dst_ref=parts.at[which, owner],
                send_sem=rsend.at[which, target], recv_sem=rrecv.at[which, owner],
                device_id=(target // n_gy, lax.rem(target, n_gy)), device_id_type=mesh_id,
            )

        @pl.loop(1, total)
        def _(step):
            move(me, lax.rem(me + step, total)).start()

        meanwhile()

        @pl.loop(1, total)
        def _(step):
            other = lax.rem(me + step, total)
            move(other, other).wait_recv()

        @pl.loop(1, total)
        def _(step):
            move(me, lax.rem(me + step, total)).wait_send()

        return jnp.sum(parts[which], axis=0)

    def assembled(table, values):
        return sum(
            table[m] * jnp.broadcast_to(values[m][0][:, values[m][1] : values[m][1] + 1], (ROWS, 128))
            for m in range(table.shape[0])
        )

    def combine(coefficients, slots, store):
        @pl.loop(0, cx)
        def _(x):
            for y in range(0, cy, 8):
                for z in range(0, cz, 128):
                    pieces = [
                        w * vecs[slot, x, y : y + 8, z : z + 128]
                        for w, slot in zip(coefficients, slots)
                    ]
                    while len(pieces) > 1:
                        pieces = [sum(pieces[i : i + 2]) for i in range(0, len(pieces), 2)]
                    store(x, y, z, pieces[0])

    @pl.loop(0, cx)
    def _(x):
        for y in range(0, cy, 8):
            for z in range(0, cz, 128):
                flatten(x, y, z, potential[x, y : y + 8, z : z + 128])

    pl.semaphore_wait(barrier, total - 1)
    run_chain(0, False)
    sums = reduced(0, lambda: levels(0, groups // 2))
    n1, n2 = 2 * s + 1, 4 * s + 1
    first = solve(assembled(first_map, [(sums, m) for m in range(n1)]), s)
    tail = [jnp.ones((8, 128), F32)] + [jnp.zeros((8, 128), F32) for _ in range(s)]
    for k in range(s):
        tail[k] = tail[k] - first[k]
        tail[k + 1] = tail[k + 1] + 0.5 * first[k]
        tail[abs(k - 1)] = tail[abs(k - 1)] + 0.5 * first[k]
    base = s + 2

    def keep(x, y, z, value):
        vecs[base + 1, x, y : y + 8, z : z + 128] = value

    combine(tail, range(1, s + 2), keep)
    for x in range(cx):
        ybuf[base + 1, 0, x : x + 1, :] = vecs[base + 1, x, 0:1, :]
        ybuf[base + 1, 1, x : x + 1, :] = vecs[base + 1, x, cy - 1 : cy, :]
    run_chain(base, True)
    again = reduced(1, lambda: levels(groups // 2, groups))
    values = [(again, m) for m in range(n2)] + [(sums, m) for m in range(n1)]
    second = solve(assembled(second_map, values), 2 * s)
    weights = [first[k] + second[k] for k in range(s)] + second[s:]

    def emit(x, y, z, value):
        out[x, y : y + 8, z : z + 128] = value
        flatten(x, y, z, value)

    combine(weights, list(range(1, s + 1)) + list(range(base + 1, base + s + 1)), emit)

    @pl.loop(0, n_gy)
    def _(peer):
        live = count[peer]
        for part in range(wide):
            group = peer * wide + part
            at = level[pl.ds(group, 1), :]
            rising = jnp.exp(0.4 * at)
            falling = jnp.exp(-0.6 * at)
            slope = 0.4 * rising + 0.6 * falling
            current = (rising - falling) + slope * gathered(flat, group)
            sent[peer, part : part + 1, :] = jnp.where(
                lane + 128 * part < live, 0.5 * current, 0.0
            )

    def link(owner, peer):
        return pltpu.make_async_remote_copy(
            src_ref=sent.at[peer], dst_ref=got.at[owner], send_sem=lsend.at[peer],
            recv_sem=lrecv.at[owner], device_id=(gx, peer), device_id_type=mesh_id,
        )

    @pl.loop(1, n_gy)
    def _(step):
        link(gy, lax.rem(gy + step, n_gy)).start()

    got[gy] = sent[gy]

    @pl.loop(1, n_gy)
    def _(step):
        other = lax.rem(gy + step, n_gy)
        link(other, other).wait_recv()

    own = particle.shape[1]
    sub = lax.broadcasted_iota(jnp.int32, (128, 128), 0)
    for start in range(0, own, 128):
        def add(peer, acc):
            for part in range(wide):
                spot = target[pl.ds(peer * wide + part, 1), :]
                acc = acc + jnp.where(spot - start == sub, got[peer, part : part + 1, :], 0.0)
            return acc

        acc = lax.fori_loop(0, n_gy, add, jnp.zeros((128, 128), F32))
        particle[:, start : start + 128] = jnp.sum(acc.T, axis=0, keepdims=True)

    @pl.loop(1, n_gy)
    def _(step):
        link(gy, lax.rem(gy + step, n_gy)).wait_send()


def shards(sizes, source, voxel_phase, lin_potential, link_voxel, link_count, link_target):
    cx, cy, cz = source.shape
    total = sizes[0] * sizes[1]
    slots = 2 * HALF + 4
    first_map, second_map = gram_maps()
    lanes = 4 * HALF + 8
    whole = pl.BlockSpec(memory_space=pltpu.VMEM)
    peers = link_count.shape[2]
    groups = link_voxel.shape[2] // 128
    scalars = pl.BlockSpec(memory_space=pltpu.SMEM)
    values, totals = pl.pallas_call(
        functools.partial(kernel, sizes),
        out_shape=(
            jax.ShapeDtypeStruct(source.shape, F32),
            jax.ShapeDtypeStruct((1, PART_DEV), F32),
        ),
        in_specs=[whole] * 5 + [scalars, scalars, whole],
        out_specs=(whole, whole),
        scratch_shapes=[
            pltpu.VMEM((slots, cx, cy, cz), F32),
            pltpu.VMEM((cx, cy, cz), F32),
            pltpu.VMEM((cx, cy, cz), F32),
            pltpu.VMEM((slots, 2, cy, cz), F32),
            pltpu.VMEM((slots, 2, cx, cz), F32),
            pltpu.VMEM((slots, 2, cx, cz), F32),
            pltpu.VMEM((lanes, 8, cz), F32),
            pltpu.VMEM((2, 1, 128), F32),
            pltpu.VMEM((2, total, 1, 128), F32),
            pltpu.VMEM((128, 128), F32),
            pltpu.VMEM((cx * cy * (cz // 128), 128), F32),
            pltpu.VMEM((groups, 128), F32),
            pltpu.VMEM((peers, groups // peers, 128), F32),
            pltpu.VMEM((peers, groups // peers, 128), F32),
            pltpu.SemaphoreType.DMA((slots, 4)),
            pltpu.SemaphoreType.DMA((slots, 4)),
            pltpu.SemaphoreType.DMA((2, total)),
            pltpu.SemaphoreType.DMA((2, total)),
            pltpu.SemaphoreType.DMA((peers,)),
            pltpu.SemaphoreType.DMA((peers,)),
        ],
        compiler_params=pltpu.CompilerParams(collective_id=0, has_side_effects=True),
    )(
        source, voxel_phase, lin_potential, jnp.asarray(first_map), jnp.asarray(second_map),
        link_voxel[0, 0], link_count[0, 0], link_target[0, 0].reshape(groups, 128),
    )
    return values, totals.reshape(1, 1, PART_DEV)


def solution(mesh):
    spec = P("gx", "gy", None)
    return jax.shard_map(
        functools.partial(shards, (mesh.shape["gx"], mesh.shape["gy"])),
        mesh=mesh,
        in_specs=(spec,) * 6,
        out_specs=(spec, spec),
        check_vma=False,
    )
```
